256 devices in a mesh: seq: 8 (over z), head: 32 (over y, x, core).
Axes of the slice: x: 4, y: 4, z: 8, core: 2. Of those that a mesh axis runs over, the one named last changes fastest.
Arguments:
- queries: bfloat16 [4096, 32, 128], P(('seq', 'head')), may hold values from -6 to 6
- keys: bfloat16 [4096, 32, 128], P(('seq', 'head')), may hold values from -6 to 6
- values: bfloat16 [4096, 32, 128], P(('seq', 'head')), may hold values from -6 to 6
- out_grad: bfloat16 [4096, 32, 128], P(('seq', 'head')), may hold values from -1.5 to 1.5
- level_weights: float32 [32, 13, 4096], P('head', None, 'seq'), may hold values from 0.2 to 2
Outputs:
- query_grad: bfloat16 [4096, 32, 128], P(('seq', 'head'))
- key_grad: bfloat16 [4096, 32, 128], P(('seq', 'head'))
- value_grad: bfloat16 [4096, 32, 128], P(('seq', 'head'))
- weight_grad: float32 [32, 13, 4096], P('head', None, 'seq')
The draws below stay inside these ranges and needn't reach their ends.
All inputs are finite; a program needn't handle non-finite values.
Results may differ from the reference program's by a relative error of at most 0.0052.
Values may be sent and summed in bfloat16 or wider, within the bound.
No kernel may reach another device: no remote copies, remote signals or barrier semaphores. Data moves between devices by JAX's collectives and lax.ppermute only.
A program may use at most 64 MiB of HBM per device.

```python
import math
import jax
import jax.numpy as jnp
from jax import lax

HEADS = 32
DK = 128
TOK_DEV = 512
TOKENS = 4096
LEVELS = 13


def steps_of(key, dims, cuts, least, largest):
    level, own = 1.0, jax.random.fold_in(key, 6)
    for dim, parts in cuts:
        steps = jnp.exp(jax.random.uniform(jax.random.fold_in(own, dim), (parts,), jnp.float32, least / len(cuts), largest / len(cuts)))
        level = level * jnp.repeat(steps, dims[dim] // parts).reshape([-1 if axis == dim else 1 for axis in range(len(dims))])
    return level


def bell_draw(stream_key, dims, scale, limit, cuts=(), held_as=jnp.bfloat16):
    factor_of = steps_of(stream_key, dims, cuts, -0.22, 0.18) if cuts else 1.0
    values = jax.random.normal(stream_key, dims, jnp.float32) * scale * factor_of
    return jnp.minimum(jnp.maximum(values, -limit), limit).astype(held_as)


def setup_inputs(seed: int = 0) -> dict:
    arg_keys = jax.random.split(jax.random.key(seed), 6)
    queries = bell_draw(arg_keys[0], (TOKENS, HEADS, DK), 1.0, 6.0, ((0, 256),))
    keys = bell_draw(arg_keys[1], (TOKENS, HEADS, DK), 1.0, 6.0, ((0, 256),))
    values = bell_draw(arg_keys[2], (TOKENS, HEADS, DK), 1.0, 6.0, ((0, 256),))
    out_grad = bell_draw(arg_keys[3], (TOKENS, HEADS, DK), 0.25, 1.5, ((0, 256),))
    level_weights = jnp.clip(jnp.exp(math.log(2.0) - 2.3025851 * jax.random.uniform(arg_keys[4], (HEADS, LEVELS, TOKENS), jnp.float32) ** steps_of(arg_keys[4], (HEADS, LEVELS, TOKENS), ((0, 32), (2, 8)), -0.2, 0.2)), 0.2, 2.0)
    return dict(queries=queries, keys=keys, values=values, out_grad=out_grad, level_weights=level_weights)


def bit_length(values, number):
    running = jnp.zeros(values.shape, jnp.int32)
    for exponent in range(number):
        running = running + (values >= 2 ** exponent).astype(jnp.int32)
    return running

def level_factors(number):
    base_scale = 1.0 / math.sqrt(DK)
    factors = [base_scale] + [base_scale * 2.0 ** (-(degree - 1) / 2.0) for degree in range(1, number)]
    return jnp.array(factors, jnp.float32)

def near_block(inputs):
    query_rows, key_rows, value_rows, grad_rows, weight_rows = inputs
    local_count = weight_rows.shape[0]
    positions = jnp.arange(TOK_DEV, dtype=jnp.int32)
    crossed = jnp.bitwise_xor(positions[:, None], positions[None, :])
    levels = bit_length(crossed, local_count - 1)
    causal = positions[None, :] <= positions[:, None]
    factors = level_factors(local_count)
    picked = jnp.take_along_axis(weight_rows.T, levels, axis=1)
    weights = jnp.where(causal, factors[levels] * picked, 0.0)
    scores = jnp.dot(query_rows, key_rows.T, preferred_element_type=jnp.float32)
    pulls = jnp.dot(grad_rows, value_rows.T, preferred_element_type=jnp.float32)
    near_scaled = (weights * scores).astype(jnp.bfloat16)
    near_pulled = (weights * pulls).astype(jnp.bfloat16)
    value_part = jnp.dot(near_scaled.T, grad_rows, preferred_element_type=jnp.float32)
    query_part = jnp.dot(near_pulled, key_rows, preferred_element_type=jnp.float32)
    key_part = jnp.dot(near_pulled.T, query_rows, preferred_element_type=jnp.float32)
    product = jnp.where(causal, scores * pulls, 0.0)
    weight_part = jnp.stack([factors[degree] * lax.optimization_barrier(jnp.sum(jnp.where(levels == degree, product, 0.0), axis=1)) for degree in range(local_count)])
    return (query_part, key_part, value_part, weight_part)

def one_head(inputs):
    queries, keys, values, out_grad, level_weights = inputs
    blocks = TOKENS // TOK_DEV
    local_count = TOK_DEV.bit_length()
    far_count = LEVELS - local_count
    query_blocks = queries.reshape(blocks, TOK_DEV, DK)
    key_blocks = keys.reshape(blocks, TOK_DEV, DK)
    value_blocks = values.reshape(blocks, TOK_DEV, DK)
    grad_blocks = out_grad.reshape(blocks, TOK_DEV, DK)
    near_weights = level_weights[:local_count].reshape(local_count, blocks, TOK_DEV).transpose(1, 0, 2)
    query_near, key_near, value_near, weight_near = lax.map(near_block, (query_blocks, key_blocks, value_blocks, grad_blocks, near_weights))
    query_wide = query_blocks.astype(jnp.float32)
    key_wide = key_blocks.astype(jnp.float32)
    value_wide = value_blocks.astype(jnp.float32)
    grad_wide = grad_blocks.astype(jnp.float32)
    factors = level_factors(LEVELS)[local_count:]
    far_weights = level_weights[local_count:].reshape(far_count, blocks, TOK_DEV)
    coefficient = factors[:, None, None] * far_weights
    pair_state = jnp.einsum('mcd,mce->mde', key_wide, value_wide, precision=lax.Precision.HIGHEST)
    scaled_grad = (coefficient[..., None] * grad_wide[None]).astype(jnp.bfloat16)
    query_state = jnp.einsum('mcd,jmce->jmde', query_wide, scaled_grad.astype(jnp.float32), precision=lax.Precision.HIGHEST)
    indices = jnp.arange(blocks, dtype=jnp.int32)
    crossed = jnp.bitwise_xor(indices[:, None], indices[None, :])
    first_bit = bit_length(crossed, far_count)
    degrees = jnp.arange(far_count, dtype=jnp.int32)[:, None, None] + 1
    lower_mask = ((first_bit[None] == degrees) & (indices[None, None, :] < indices[None, :, None])).astype(jnp.float32)
    upper_mask = ((first_bit[None] == degrees) & (indices[None, None, :] > indices[None, :, None])).astype(jnp.float32)
    lower_state = jnp.einsum('jmn,nde->jmde', lower_mask, pair_state, precision=lax.Precision.HIGHEST).astype(jnp.bfloat16)
    upper_sum = lax.optimization_barrier(jnp.sum(jnp.einsum('jmn,jnde->jmde', upper_mask, query_state, precision=lax.Precision.HIGHEST), axis=0)).astype(jnp.bfloat16)
    far_update = jnp.einsum('mce,jmde->jmcd', grad_wide, lower_state.astype(jnp.float32), precision=lax.Precision.HIGHEST)
    query_grad = (query_near + lax.optimization_barrier(jnp.sum(coefficient[..., None] * far_update, axis=0))).astype(jnp.bfloat16)
    upper_wide = upper_sum.astype(jnp.float32)
    key_grad = (key_near + jnp.einsum('mce,mde->mcd', value_wide, upper_wide, precision=lax.Precision.HIGHEST)).astype(jnp.bfloat16)
    value_grad = (value_near + jnp.einsum('mcd,mde->mce', key_wide, upper_wide, precision=lax.Precision.HIGHEST)).astype(jnp.bfloat16)
    weight_far = factors[:, None, None] * lax.optimization_barrier(jnp.sum(query_wide[None] * far_update, axis=-1))
    weight_grad = jnp.concatenate([weight_near.transpose(1, 0, 2).reshape(local_count, TOKENS), weight_far.reshape(far_count, TOKENS)], axis=0)
    return (query_grad.reshape(TOKENS, DK), key_grad.reshape(TOKENS, DK), value_grad.reshape(TOKENS, DK), weight_grad)

def reference(queries, keys, values, out_grad, level_weights):
    head_major = tuple((jnp.moveaxis(member, 1, 0) for member in (queries, keys, values, out_grad)))
    query_grad, key_grad, value_grad, weight_grad = lax.map(one_head, head_major + (level_weights,))
    return (jnp.moveaxis(query_grad, 0, 1), jnp.moveaxis(key_grad, 0, 1), jnp.moveaxis(value_grad, 0, 1), weight_grad)
```

```python
import math

import jax
import jax.numpy as jnp
from jax import lax
from jax.experimental import pallas as pl
from jax.experimental.pallas import tpu as pltpu
from jax.sharding import PartitionSpec as P

HEAD_AXIS = "head"
SEQ_AXIS = "seq"
LANES = 128
F32 = jnp.float32
BF16 = jnp.bfloat16


def level_factor(degree, head_width):
    base_scale = 1.0 / math.sqrt(head_width)
    if degree == 0:
        return base_scale
    return base_scale * 2.0 ** (-(degree - 1) / 2.0)


def dot_nn(left, right):
    return lax.dot_general(left, right, (((1,), (0,)), ((), ())), preferred_element_type=F32)


def dot_nt(left, right):
    return lax.dot_general(left, right, (((1,), (1,)), ((), ())), preferred_element_type=F32)


def transposed(rows):
    return jnp.transpose(rows.astype(F32))


def seq_bit(degree):
    return (lax.axis_index(SEQ_AXIS) >> degree) & 1 == 1


def call(body, out_shape, operands, scratch=(), flops=0, moved=0):
    return pl.pallas_call(
        body,
        out_shape=out_shape,
        scratch_shapes=list(scratch),
        cost_estimate=pl.CostEstimate(flops=flops, bytes_accessed=moved, transcendentals=0),
    )(*operands)


def pack(members):
    rows, heads, width = members[0].shape
    count = len(members)

    def body(*refs):
        ins, out, wide = refs[:count], refs[count], refs[count + 1]
        for index in range(count):
            wide[index] = ins[index][...].astype(F32).reshape(rows * heads, width)
        for index in range(count):
            for head in range(heads):
                piece = wide[index, pl.ds(head, rows, stride=heads), :]
                out[head, index * rows : (index + 1) * rows, :] = piece.astype(BF16)

    size = count * rows * heads * width
    return call(
        body,
        jax.ShapeDtypeStruct((heads, count * rows, width), BF16),
        members,
        [pltpu.VMEM((count, rows * heads, width), F32)],
        moved=4 * size,
    )


def unpack(joined, count):
    heads, total, width = joined.shape
    rows = total // count

    def body(joined_ref, *refs):
        outs, wide = refs[:count], refs[count]
        for index in range(count):
            for head in range(heads):
                piece = joined_ref[head, index * rows : (index + 1) * rows, :]
                wide[index, pl.ds(head, rows, stride=heads), :] = piece.astype(F32)
        for index in range(count):
            outs[index][...] = wide[index].reshape(rows, heads, width).astype(BF16)

    size = count * rows * heads * width
    return call(
        body,
        tuple(jax.ShapeDtypeStruct((rows, heads, width), BF16) for _ in range(count)),
        (joined,),
        [pltpu.VMEM((count, rows * heads, width), F32)],
        moved=4 * size,
    )


def part(ref, index, chunk):
    sources, _, width = ref.shape
    return ref[:, index * chunk : (index + 1) * chunk, :].reshape(sources * chunk, width)


def block_states(rows_in, weights, chunk, first_far, far_count):
    width = rows_in.shape[2]

    def body(rows_ref, weight_ref, near_ref, wide_ref):
        query, key, value, grad = (part(rows_ref, index, chunk) for index in range(4))
        query_t = transposed(query)
        pair = dot_nn(transposed(key).astype(BF16), value)
        messages = []
        for degree in range(far_count):
            level = first_far + degree
            scale = level_factor(level, width) * weight_ref[level]
            state = dot_nn((scale * query_t).astype(BF16), grad)
            messages.append(jnp.where(seq_bit(degree), state, pair).astype(BF16))
        near_ref[0] = messages[0]
        near_ref[1] = messages[2]
        wide_ref[0] = messages[1]
        wide_ref[1] = messages[2]

    shape = jax.ShapeDtypeStruct((2, width, width), BF16)
    return call(body, (shape, shape), (rows_in, weights), flops=10**8, moved=10**6)


def near_terms(rows_in, weights, chunk, near_count):
    sources, _, width = rows_in.shape
    tokens = sources * chunk
    pieces = tokens // LANES
    inner = LANES.bit_length()

    def body(rows_ref, weight_ref, query_ref, key_ref, value_ref, grad_weight_ref):
        query, key, value, grad = (part(rows_ref, index, chunk) for index in range(4))
        scale = [level_factor(level, width) * weight_ref[level] for level in range(near_count)]
        source = lax.broadcasted_iota(jnp.int32, (LANES, LANES), 0)
        target = lax.broadcasted_iota(jnp.int32, (LANES, LANES), 1)
        crossed = source ^ target
        level_of = jnp.where(source <= target, 0, 64)
        for level in range(1, inner):
            level_of = level_of + (crossed >= 2 ** (level - 1)).astype(jnp.int32)
        masks = [level_of == level for level in range(inner)]
        sums = [[None] * pieces for _ in range(near_count)]
        key_t = transposed(key).astype(BF16)
        for low in range(pieces):
            begin = low * LANES
            span = tokens - begin
            scores = dot_nt(key[begin : begin + LANES], query[begin:])
            pulls = dot_nt(value[begin : begin + LANES], grad[begin:])
            product = scores * pulls
            inside = jnp.zeros((LANES, LANES), F32)
            corner = product[:, :LANES]
            for level in range(inner):
                row = scale[level][:, begin : begin + LANES]
                inside = jnp.where(masks[level], row, inside)
                sums[level][low] = jnp.sum(
                    jnp.where(masks[level], corner, 0.0), axis=0, keepdims=True
                )
            columns = [inside]
            for high in range(low + 1, pieces):
                level = (low ^ high).bit_length() + inner - 1
                left = (high - low) * LANES
                row = scale[level][:, high * LANES : (high + 1) * LANES]
                columns.append(jnp.broadcast_to(row, (LANES, LANES)))
                added = jnp.sum(product[:, left : left + LANES], axis=0, keepdims=True)
                held = sums[level][high]
                sums[level][high] = added if held is None else held + added
            weight = jnp.concatenate(columns, axis=1)
            scaled = (weight * scores).astype(BF16)
            pulled = (weight * pulls).astype(BF16)
            value_ref[begin : begin + LANES, :] = dot_nn(scaled, grad[begin:])
            key_ref[begin : begin + LANES, :] = dot_nn(pulled, query[begin:])
            partial = dot_nn(key_t[:, begin : begin + LANES], pulled)
            if low == 0:
                query_ref[...] = partial
            else:
                query_ref[:, begin:] = query_ref[:, begin:] + partial
        zero = jnp.zeros((1, LANES), F32)
        for level in range(near_count):
            row = jnp.concatenate([zero if item is None else item for item in sums[level]], axis=1)
            grad_weight_ref[level] = level_factor(level, width) * row

    return call(
        body,
        (
            jax.ShapeDtypeStruct((width, tokens), F32),
            jax.ShapeDtypeStruct((tokens, width), F32),
            jax.ShapeDtypeStruct((tokens, width), F32),
            jax.ShapeDtypeStruct((near_count, 1, tokens), F32),
        ),
        (rows_in, weights),
        flops=4 * 10**8,
        moved=3 * 10**6,
    )


def join_far(rows_in, weights, near, received, chunk, first_far, far_count):
    sources, _, width = rows_in.shape
    tokens = sources * chunk
    levels = weights.shape[0]
    query_near, key_near, value_near, weight_near = near

    def body(
        rows_ref,
        weight_ref,
        query_ref,
        key_ref,
        value_ref,
        near_weight_ref,
        first_ref,
        second_ref,
        third_ref,
        fourth_ref,
        out_ref,
        grad_weight_ref,
    ):
        query, key, value, grad = (part(rows_ref, index, chunk) for index in range(4))
        sums = [
            first_ref[0].astype(F32),
            second_ref[0].astype(F32) + third_ref[0].astype(F32),
            fourth_ref[0].astype(F32),
        ]
        query_t = transposed(query)
        total = query_ref[...]
        upper = jnp.zeros((width, width), F32)
        for degree in range(far_count):
            level = first_far + degree
            bit = seq_bit(degree)
            lower = jnp.where(bit, sums[degree], 0.0).astype(BF16)
            upper = upper + jnp.where(bit, 0.0, sums[degree])
            update = dot_nt(lower, grad)
            factor = level_factor(level, width)
            total = total + (factor * weight_ref[level]) * update
            grad_weight_ref[level] = factor * jnp.sum(query_t * update, axis=0, keepdims=True)
        for level in range(first_far):
            grad_weight_ref[level] = near_weight_ref[level]
        upper = upper.astype(BF16)
        results = (
            jnp.transpose(total),
            key_ref[...] + dot_nt(value, upper),
            value_ref[...] + dot_nn(key, upper),
        )
        for index, result in enumerate(results):
            out_ref[:, index * chunk : (index + 1) * chunk, :] = result.astype(BF16).reshape(
                sources, chunk, width
            )

    return call(
        body,
        (
            jax.ShapeDtypeStruct((sources, 3 * chunk, width), BF16),
            jax.ShapeDtypeStruct((levels, 1, tokens), F32),
        ),
        (rows_in, weights, query_near, key_near, value_near, weight_near, *received),
        flops=2 * 10**8,
        moved=3 * 10**6,
    )


def partner(value, mask):
    size = lax.axis_size(SEQ_AXIS)
    return lax.ppermute(value, SEQ_AXIS, [(place, place ^ mask) for place in range(size)])


def on_device(queries, keys, values, out_grad, level_weights):
    chunk = queries.shape[0]
    weights = jnp.transpose(level_weights, (1, 0, 2))
    sent = pack((queries, keys, values, out_grad))
    rows = lax.all_to_all(sent, HEAD_AXIS, 0, 0, tiled=True)
    first_far = weights.shape[2].bit_length()
    far_count = weights.shape[0] - first_far
    near_pair, wide_pair = block_states(rows, weights, chunk, first_far, far_count)
    near = near_terms(rows, weights, chunk, first_far)
    first = partner(near_pair, 1)
    second = partner(wide_pair, 2)
    third = partner(wide_pair, 3)
    quad = near_pair[1:] + first[1:] + second[1:] + third[1:]
    fourth = partner(quad, 7)
    joined, grad_weights = join_far(
        rows, weights, near, (first, second, third, fourth), chunk, first_far, far_count
    )
    back = lax.all_to_all(joined, HEAD_AXIS, 0, 0, tiled=True)
    query_out, key_out, value_out = unpack(back, 3)
    return (query_out, key_out, value_out, jnp.transpose(grad_weights, (1, 0, 2)))


def solution(mesh):
    rows = P((SEQ_AXIS, HEAD_AXIS), None, None)
    levels = P(HEAD_AXIS, None, SEQ_AXIS)
    return jax.shard_map(
        on_device,
        mesh=mesh,
        in_specs=(rows, rows, rows, rows, levels),
        out_specs=(rows, rows, rows, levels),
        check_vma=False,
    )
```

```python
import math

import jax
import jax.numpy as jnp
from jax import lax
from jax.experimental import pallas as pl
from jax.experimental.pallas import tpu as pltpu
from jax.sharding import PartitionSpec as P


HEAD_AXIS = "head"
SEQ_AXIS = "seq"
LANES = 128
F32 = jnp.float32
BF16 = jnp.bfloat16


def level_factor(degree, head_width):
    base_scale = 1.0 / math.sqrt(head_width)
    if degree == 0:
        return base_scale
    return base_scale * 2.0 ** (-(degree - 1) / 2.0)


def dot_nn(left, right):
    return lax.dot_general(left, right, (((1,), (0,)), ((), ())), preferred_element_type=F32)


def dot_nt(left, right):
    return lax.dot_general(left, right, (((1,), (1,)), ((), ())), preferred_element_type=F32)


def transposed(rows):
    return jnp.transpose(rows.astype(F32))


def seq_bit(degree):
    return (lax.axis_index(SEQ_AXIS) >> degree) & 1 == 1


def call(
    body,
    out_shape,
    operands,
    scratch=(),
    flops=0,
    moved=0,
    in_space=pltpu.VMEM,
    out_space=pltpu.VMEM,
    limit=16 * 2**20,
):
    return pl.pallas_call(
        body,
        out_shape=out_shape,
        in_specs=[pl.BlockSpec(memory_space=in_space)] * len(operands),
        out_specs=jax.tree.map(lambda _: pl.BlockSpec(memory_space=out_space), out_shape),
        scratch_shapes=list(scratch),
        compiler_params=pltpu.CompilerParams(vmem_limit_bytes=limit),
        cost_estimate=pl.CostEstimate(flops=flops, bytes_accessed=moved, transcendentals=0),
    )(*operands)


def pack(members):
    rows, heads, width = members[0].shape
    count = len(members)

    def body(*refs):
        ins, out = refs[:count], refs[count]
        narrow, wide, sems = refs[count + 1 :]
        copies = [
            pltpu.make_async_copy(ins[index], narrow.at[index], sems.at[index])
            for index in range(count)
        ]
        for copy in copies:
            copy.start()
        for index in range(count):
            copies[index].wait()
            wide[index] = narrow[index].astype(F32).reshape(rows * heads, width)
            for head in range(heads):
                piece = wide[index, pl.ds(head, rows, stride=heads), :]
                out[head, index * rows : (index + 1) * rows, :] = piece.astype(BF16)

    size = count * rows * heads * width
    return call(
        body,
        jax.ShapeDtypeStruct((heads, count * rows, width), BF16),
        members,
        [
            pltpu.VMEM((count, rows, heads, width), BF16),
            pltpu.VMEM((count, rows * heads, width), F32),
            pltpu.SemaphoreType.DMA((count,)),
        ],
        moved=4 * size,
        in_space=pltpu.HBM,
        limit=63 * 2**20,
    )


def unpack(joined, count):
    heads, total, width = joined.shape
    rows = total // count

    def body(joined_ref, *refs):
        outs = refs[:count]
        narrow, wide, sems = refs[count:]
        copies = []
        for index in range(count):
            for head in range(heads):
                piece = joined_ref[head, index * rows : (index + 1) * rows, :]
                wide[index, pl.ds(head, rows, stride=heads), :] = piece.astype(F32)
            narrow[index] = wide[index].reshape(rows, heads, width).astype(BF16)
            copy = pltpu.make_async_copy(narrow.at[index], outs[index], sems.at[index])
            copy.start()
            copies.append(copy)
        for copy in copies:
            copy.wait()

    size = count * rows * heads * width
    return call(
        body,
        tuple(jax.ShapeDtypeStruct((rows, heads, width), BF16) for _ in range(count)),
        (joined,),
        [
            pltpu.VMEM((count, rows, heads, width), BF16),
            pltpu.VMEM((count, rows * heads, width), F32),
            pltpu.SemaphoreType.DMA((count,)),
        ],
        moved=4 * size,
        out_space=pltpu.HBM,
    )


def part(ref, index, chunk):
    sources, _, width = ref.shape
    return ref[:, index * chunk : (index + 1) * chunk, :].reshape(sources * chunk, width)


def block_states(rows_in, weights, chunk, first_far, far_count):
    width = rows_in.shape[2]

    def body(rows_ref, weight_ref, *message_refs):
        query, key, value, grad = (part(rows_ref, index, chunk) for index in range(4))
        query_t = transposed(query)
        pair = dot_nn(transposed(key).astype(BF16), value)
        messages = []
        for degree in range(far_count):
            level = first_far + degree
            scale = level_factor(level, width) * weight_ref[level]
            state = dot_nn((scale * query_t).astype(BF16), grad)
            messages.append(jnp.where(seq_bit(degree), state, pair).astype(BF16))
        for refs, groups in zip(message_refs, SENT):
            for slot, degree in enumerate(groups):
                refs[slot] = messages[degree]

    shapes = tuple(jax.ShapeDtypeStruct((len(groups), width, width), BF16) for groups in SENT)
    return call(body, shapes, (rows_in, weights), flops=10**8, moved=10**6)


def near_terms(rows_in, weights, chunk, near_count):
    sources, _, width = rows_in.shape
    tokens = sources * chunk
    pieces = tokens // LANES
    inner = LANES.bit_length()

    def body(rows_ref, weight_ref, query_ref, key_ref, value_ref, grad_weight_ref):
        query, key, value, grad = (part(rows_ref, index, chunk) for index in range(4))
        scale = [level_factor(level, width) * weight_ref[level] for level in range(near_count)]
        source = lax.broadcasted_iota(jnp.int32, (LANES, LANES), 0)
        target = lax.broadcasted_iota(jnp.int32, (LANES, LANES), 1)
        crossed = source ^ target
        level_of = jnp.where(source <= target, 0, 64)
        for level in range(1, inner):
            level_of = level_of + (crossed >= 2 ** (level - 1)).astype(jnp.int32)
        masks = [level_of == level for level in range(inner)]
        sums = [[None] * pieces for _ in range(near_count)]
        key_t = transposed(key).astype(BF16)
        for low in range(pieces):
            begin = low * LANES
            scores = dot_nt(key[begin : begin + LANES], query[begin:])
            pulls = dot_nt(value[begin : begin + LANES], grad[begin:])
            product = scores * pulls
            inside = jnp.zeros((LANES, LANES), F32)
            corner = product[:, :LANES]
            for level in range(inner):
                row = scale[level][:, begin : begin + LANES]
                inside = jnp.where(masks[level], row, inside)
                sums[level][low] = jnp.sum(
                    jnp.where(masks[level], corner, 0.0), axis=0, keepdims=True
                )
            columns = [inside]
            for high in range(low + 1, pieces):
                level = (low ^ high).bit_length() + inner - 1
                left = (high - low) * LANES
                row = scale[level][:, high * LANES : (high + 1) * LANES]
                columns.append(jnp.broadcast_to(row, (LANES, LANES)))
                added = jnp.sum(product[:, left : left + LANES], axis=0, keepdims=True)
                held = sums[level][high]
                sums[level][high] = added if held is None else held + added
            weight = jnp.concatenate(columns, axis=1)
            scaled = (weight * scores).astype(BF16)
            pulled = (weight * pulls).astype(BF16)
            value_ref[begin : begin + LANES, :] = dot_nn(scaled, grad[begin:])
            key_ref[begin : begin + LANES, :] = dot_nn(pulled, query[begin:])
            partial = dot_nn(key_t[:, begin : begin + LANES], pulled)
            if low == 0:
                query_ref[...] = partial
            else:
                query_ref[:, begin:] = query_ref[:, begin:] + partial
        zero = jnp.zeros((1, LANES), F32)
        for level in range(near_count):
            row = jnp.concatenate([zero if item is None else item for item in sums[level]], axis=1)
            grad_weight_ref[level] = level_factor(level, width) * row

    return call(
        body,
        (
            jax.ShapeDtypeStruct((width, tokens), F32),
            jax.ShapeDtypeStruct((tokens, width), F32),
            jax.ShapeDtypeStruct((tokens, width), F32),
            jax.ShapeDtypeStruct((near_count, 1, tokens), F32),
        ),
        (rows_in, weights),
        flops=4 * 10**8,
        moved=3 * 10**6,
    )


def join_far(rows_in, weights, near, received, chunk, first_far, far_count):
    sources, _, width = rows_in.shape
    tokens = sources * chunk
    levels = weights.shape[0]
    query_near, key_near, value_near, weight_near = near

    def body(
        rows_ref,
        weight_ref,
        query_ref,
        key_ref,
        value_ref,
        near_weight_ref,
        *refs,
    ):
        message_refs, (out_ref, grad_weight_ref) = refs[:-2], refs[-2:]
        query, key, value, grad = (part(rows_ref, index, chunk) for index in range(4))
        sums = []
        for sources_of in TAKEN:
            terms = [message_refs[place][slot].astype(F32) for place, slot in sources_of]
            total = terms[0]
            for term in terms[1:]:
                total = total + term
            sums.append(total)
        query_t = transposed(query)
        total = query_ref[...]
        upper = jnp.zeros((width, width), F32)
        for degree in range(far_count):
            level = first_far + degree
            bit = seq_bit(degree)
            lower = jnp.where(bit, sums[degree], 0.0).astype(BF16)
            upper = upper + jnp.where(bit, 0.0, sums[degree])
            update = dot_nt(lower, grad)
            factor = level_factor(level, width)
            total = total + (factor * weight_ref[level]) * update
            grad_weight_ref[level] = factor * jnp.sum(query_t * update, axis=0, keepdims=True)
        for level in range(first_far):
            grad_weight_ref[level] = near_weight_ref[level]
        upper = upper.astype(BF16)
        results = (
            jnp.transpose(total),
            key_ref[...] + dot_nt(value, upper),
            value_ref[...] + dot_nn(key, upper),
        )
        for index, result in enumerate(results):
            out_ref[:, index * chunk : (index + 1) * chunk, :] = result.astype(BF16).reshape(
                sources, chunk, width
            )

    return call(
        body,
        (
            jax.ShapeDtypeStruct((sources, 3 * chunk, width), BF16),
            jax.ShapeDtypeStruct((levels, 1, tokens), F32),
        ),
        (rows_in, weights, query_near, key_near, value_near, weight_near, *received),
        flops=2 * 10**8,
        moved=3 * 10**6,
    )


def partner(value, mask):
    size = lax.axis_size(SEQ_AXIS)
    return lax.ppermute(value, SEQ_AXIS, [(place, place ^ mask) for place in range(size)])


def on_device(queries, keys, values, out_grad, level_weights):
    chunk = queries.shape[0]
    weights = jnp.transpose(level_weights, (1, 0, 2))
    sent = pack((queries, keys, values, out_grad))
    rows = lax.all_to_all(sent, HEAD_AXIS, 0, 0, tiled=True)
    first_far = weights.shape[2].bit_length()
    far_count = weights.shape[0] - first_far
    messages = block_states(rows, weights, chunk, first_far, far_count)
    near = near_terms(rows, weights, chunk, first_far)
    received = exchange(messages)
    joined, grad_weights = join_far(
        rows, weights, near, received, chunk, first_far, far_count
    )
    back = lax.all_to_all(joined, HEAD_AXIS, 0, 0, tiled=True)
    query_out, key_out, value_out = unpack(back, 3)
    return (query_out, key_out, value_out, jnp.transpose(grad_weights, (1, 0, 2)))


SENT = ((0, 2), (1,), (2,))
TAKEN = (((0, 0),), ((1, 0), (2, 0)), ((3, 0),))


def exchange(messages):
    a, b, c = messages
    near, mid, far = partner(a, 1), partner(c, 2), partner(c, 3)
    second, third = partner(b, 2), partner(b, 3)
    quad = c + near[1:] + mid + far
    return (near, second, third, partner(quad, 7))


def solution(mesh):
    rows = P((SEQ_AXIS, HEAD_AXIS), None, None)
    levels = P(HEAD_AXIS, None, SEQ_AXIS)

    return jax.shard_map(
        on_device,
        mesh=mesh,
        in_specs=(rows, rows, rows, rows, levels),
        out_specs=(rows, rows, rows, levels),
        check_vma=False,
    )
```

```python
import math

import jax
import jax.numpy as jnp
from jax import lax
from jax.experimental import pallas as pl
from jax.experimental.pallas import tpu as pltpu
from jax.sharding import PartitionSpec as P


HEAD_AXIS = "head"
SEQ_AXIS = "seq"
LANES = 128
F32 = jnp.float32
BF16 = jnp.bfloat16


def level_factor(degree, head_width):
    base_scale = 1.0 / math.sqrt(head_width)
    if degree == 0:
        return base_scale
    return base_scale * 2.0 ** (-(degree - 1) / 2.0)


def dot_nn(left, right):
    return lax.dot_general(left, right, (((1,), (0,)), ((), ())), preferred_element_type=F32)


def dot_nt(left, right):
    return lax.dot_general(left, right, (((1,), (1,)), ((), ())), preferred_element_type=F32)


def transposed(rows):
    return jnp.transpose(rows.astype(F32))


def seq_bit(degree):
    return (lax.axis_index(SEQ_AXIS) >> degree) & 1 == 1


def call(
    body,
    out_shape,
    operands,
    scratch=(),
    flops=0,
    moved=0,
    in_space=pltpu.VMEM,
    out_space=pltpu.VMEM,
    limit=16 * 2**20,
):
    return pl.pallas_call(
        body,
        out_shape=out_shape,
        in_specs=[pl.BlockSpec(memory_space=in_space)] * len(operands),
        out_specs=jax.tree.map(lambda _: pl.BlockSpec(memory_space=out_space), out_shape),
        scratch_shapes=list(scratch),
        compiler_params=pltpu.CompilerParams(vmem_limit_bytes=limit),
        cost_estimate=pl.CostEstimate(flops=flops, bytes_accessed=moved, transcendentals=0),
    )(*operands)


def pack(members):
    rows, heads, width = members[0].shape
    count = len(members)
    members = [pltpu.with_memory_space_constraint(member, pltpu.HBM) for member in members]

    def body(*refs):
        ins, out = refs[:count], refs[count]
        narrow, _, sems = refs[count + 1 :]
        copies = [
            pltpu.make_async_copy(ins[index], narrow.at[index], sems.at[index])
            for index in range(count)
        ]
        for copy in copies:
            copy.start()
        for index in range(count):
            copies[index].wait()
            out[:, index * rows : (index + 1) * rows, :] = jnp.swapaxes(narrow[index], 0, 1)

    size = count * rows * heads * width
    return call(
        body,
        jax.ShapeDtypeStruct((heads, count * rows, width), BF16),
        members,
        [
            pltpu.VMEM((count, rows, heads, width), BF16),
            pltpu.VMEM((count, rows * heads, width), F32),
            pltpu.SemaphoreType.DMA((count,)),
        ],
        moved=4 * size,
        in_space=pltpu.HBM,
        limit=16 * 2**20,
    )


def unpack(joined, grad_weights, count):
    heads, total, width = joined.shape
    rows = total // count

    def body(joined_ref, weight_ref, *refs):
        outs, weight_out = refs[:count], refs[count]
        narrow, _, sems = refs[count + 1 :]
        copies = [pltpu.make_async_copy(weight_ref, weight_out, sems.at[count])]
        copies[0].start()
        for index in range(count):
            narrow[index] = jnp.swapaxes(joined_ref[:, index * rows : (index + 1) * rows, :], 0, 1)
            copy = pltpu.make_async_copy(narrow.at[index], outs[index], sems.at[index])
            copy.start()
            copies.append(copy)
        for copy in copies:
            copy.wait()

    size = count * rows * heads * width
    one = jax.ShapeDtypeStruct((rows, heads, width), BF16)
    return call(
        body,
        (one,) * count + (jax.ShapeDtypeStruct(grad_weights.shape, F32),),
        (joined, grad_weights),
        [
            pltpu.VMEM((count, rows, heads, width), BF16),
            pltpu.VMEM((count, heads * rows, width), F32),
            pltpu.SemaphoreType.DMA((count + 1,)),
        ],
        moved=4 * size,
        out_space=pltpu.HBM,
    )


def part(ref, index, chunk):
    sources, _, width = ref.shape
    return ref[:, index * chunk : (index + 1) * chunk, :].reshape(sources * chunk, width)


def block_states(rows_in, weights, chunk, first_far, far_count):
    width = rows_in.shape[2]

    def body(rows_ref, weight_ref, *message_refs):
        query, key, value, grad = (part(rows_ref, index, chunk) for index in range(4))
        query_t = transposed(query)
        pair = dot_nn(transposed(key).astype(BF16), value)
        messages = []
        for degree in range(far_count):
            level = first_far + degree
            scale = level_factor(level, width) * weight_ref[level]
            state = dot_nn((scale * query_t).astype(BF16), grad)
            messages.append(jnp.where(seq_bit(degree), state, pair).astype(BF16))
        for refs, groups in zip(message_refs, SENT):
            for slot, degree in enumerate(groups):
                refs[slot] = messages[degree]

    shapes = tuple(jax.ShapeDtypeStruct((len(groups), width, width), BF16) for groups in SENT)
    return call(body, shapes, (rows_in, weights), flops=10**8, moved=10**6)


def near_terms(rows_in, weights, chunk, near_count):
    sources, _, width = rows_in.shape
    tokens = sources * chunk
    pieces = tokens // LANES
    inner = LANES.bit_length()

    def body(rows_ref, weight_ref, query_ref, key_ref, value_ref, grad_weight_ref):
        query, key, value, grad = (part(rows_ref, index, chunk) for index in range(4))
        scale = [level_factor(level, width) * weight_ref[level] for level in range(near_count)]
        source = lax.broadcasted_iota(jnp.int32, (LANES, LANES), 0)
        target = lax.broadcasted_iota(jnp.int32, (LANES, LANES), 1)
        crossed = source ^ target
        level_of = jnp.where(source <= target, 0, 64)
        for level in range(1, inner):
            level_of = level_of + (crossed >= 2 ** (level - 1)).astype(jnp.int32)
        masks = [level_of == level for level in range(inner)]
        sums = [[None] * pieces for _ in range(near_count)]
        key_t = transposed(key).astype(BF16)
        for low in range(pieces):
            begin = low * LANES
            scores = dot_nt(key[begin : begin + LANES], query[begin:])
            pulls = dot_nt(value[begin : begin + LANES], grad[begin:])
            product = scores * pulls
            inside = jnp.zeros((LANES, LANES), F32)
            corner = product[:, :LANES]
            for level in range(inner):
                row = scale[level][:, begin : begin + LANES]
                inside = jnp.where(masks[level], row, inside)
                sums[level][low] = jnp.sum(
                    jnp.where(masks[level], corner, 0.0), axis=0, keepdims=True
                )
            columns = [inside]
            for high in range(low + 1, pieces):
                level = (low ^ high).bit_length() + inner - 1
                left = (high - low) * LANES
                row = scale[level][:, high * LANES : (high + 1) * LANES]
                columns.append(jnp.broadcast_to(row, (LANES, LANES)))
                added = jnp.sum(product[:, left : left + LANES], axis=0, keepdims=True)
                held = sums[level][high]
                sums[level][high] = added if held is None else held + added
            weight = jnp.concatenate(columns, axis=1)
            scaled = (weight * scores).astype(BF16)
            pulled = (weight * pulls).astype(BF16)
            value_ref[begin : begin + LANES, :] = dot_nn(scaled, grad[begin:])
            key_ref[begin : begin + LANES, :] = dot_nn(pulled, query[begin:])
            partial = dot_nn(key_t[:, begin : begin + LANES], pulled)
            if low == 0:
                query_ref[...] = partial
            else:
                query_ref[:, begin:] = query_ref[:, begin:] + partial
        zero = jnp.zeros((1, LANES), F32)
        for level in range(near_count):
            row = jnp.concatenate([zero if item is None else item for item in sums[level]], axis=1)
            grad_weight_ref[level] = level_factor(level, width) * row

    return call(
        body,
        (
            jax.ShapeDtypeStruct((width, tokens), F32),
            jax.ShapeDtypeStruct((tokens, width), F32),
            jax.ShapeDtypeStruct((tokens, width), F32),
            jax.ShapeDtypeStruct((near_count, 1, tokens), F32),
        ),
        (rows_in, weights),
        flops=4 * 10**8,
        moved=3 * 10**6,
    )


def join_far(rows_in, weights, near, received, chunk, first_far, far_count):
    sources, _, width = rows_in.shape
    tokens = sources * chunk
    levels = weights.shape[0]
    query_near, key_near, value_near, weight_near = near

    def body(
        rows_ref,
        weight_ref,
        query_ref,
        key_ref,
        value_ref,
        near_weight_ref,
        *refs,
    ):
        message_refs, (out_ref, grad_weight_ref) = refs[:-2], refs[-2:]
        query, key, value, grad = (part(rows_ref, index, chunk) for index in range(4))
        sums = []
        for sources_of in TAKEN:
            terms = [message_refs[place][slot].astype(F32) for place, slot in sources_of]
            total = terms[0]
            for term in terms[1:]:
                total = total + term
            sums.append(total)
        query_t = transposed(query)
        total = query_ref[...]
        upper = jnp.zeros((width, width), F32)
        for degree in range(far_count):
            level = first_far + degree
            bit = seq_bit(degree)
            lower = jnp.where(bit, sums[degree], 0.0).astype(BF16)
            upper = upper + jnp.where(bit, 0.0, sums[degree])
            update = dot_nt(lower, grad)
            factor = level_factor(level, width)
            total = total + (factor * weight_ref[level]) * update
            grad_weight_ref[level] = factor * jnp.sum(query_t * update, axis=0, keepdims=True)
        for level in range(first_far):
            grad_weight_ref[level] = near_weight_ref[level]
        upper = upper.astype(BF16)
        results = (
            jnp.transpose(total),
            key_ref[...] + dot_nt(value, upper),
            value_ref[...] + dot_nn(key, upper),
        )
        for index, result in enumerate(results):
            out_ref[:, index * chunk : (index + 1) * chunk, :] = result.astype(BF16).reshape(
                sources, chunk, width
            )

    return call(
        body,
        (
            jax.ShapeDtypeStruct((sources, 3 * chunk, width), BF16),
            jax.ShapeDtypeStruct((levels, 1, tokens), F32),
        ),
        (rows_in, weights, query_near, key_near, value_near, weight_near, *received),
        flops=2 * 10**8,
        moved=3 * 10**6,
    )


def partner(value, mask):
    size = lax.axis_size(SEQ_AXIS)
    return lax.ppermute(value, SEQ_AXIS, [(place, place ^ mask) for place in range(size)])


def on_device(queries, keys, values, out_grad, level_weights):
    chunk = queries.shape[0]
    weights = jnp.transpose(level_weights, (1, 0, 2))
    sent = pack((queries, keys, values, out_grad))
    rows = lax.all_to_all(sent, HEAD_AXIS, 0, 0, tiled=True)
    first_far = weights.shape[2].bit_length()
    far_count = weights.shape[0] - first_far
    messages = block_states(rows, weights, chunk, first_far, far_count)
    near = near_terms(rows, weights, chunk, first_far)
    received = exchange(messages)
    joined, grad_weights = join_far(
        rows, weights, near, received, chunk, first_far, far_count
    )
    back = lax.all_to_all(joined, HEAD_AXIS, 0, 0, tiled=True)
    query_out, key_out, value_out, grad_weights = unpack(back, grad_weights, 3)
    return (query_out, key_out, value_out, jnp.transpose(grad_weights, (1, 0, 2)))


SENT = ((0, 2), (1,), (2,))
TAKEN = (((0, 0),), ((1, 0), (2, 0)), ((3, 0),))


def exchange(messages):
    a, b, c = messages
    near, mid, far = partner(a, 1), partner(c, 2), partner(c, 3)
    second, third = partner(b, 2), partner(b, 3)
    quad = c + near[1:] + mid + far
    return (near, second, third, partner(quad, 7))


def solution(mesh):
    rows = P((SEQ_AXIS, HEAD_AXIS), None, None)
    levels = P(HEAD_AXIS, None, SEQ_AXIS)

    return jax.shard_map(
        on_device,
        mesh=mesh,
        in_specs=(rows, rows, rows, rows, levels),
        out_specs=(rows, rows, rows, levels),
        check_vma=False,
    )
```

```python
import math

import jax
import jax.numpy as jnp
from jax import lax
from jax.experimental import pallas as pl
from jax.experimental.pallas import tpu as pltpu
from jax.sharding import PartitionSpec as P


HEAD_AXIS = "head"
SEQ_AXIS = "seq"
LANES = 128
F32 = jnp.float32
BF16 = jnp.bfloat16


def level_factor(degree, head_width):
    base_scale = 1.0 / math.sqrt(head_width)
    if degree == 0:
        return base_scale
    return base_scale * 2.0 ** (-(degree - 1) / 2.0)


def dot_nn(left, right):
    return lax.dot_general(left, right, (((1,), (0,)), ((), ())), preferred_element_type=F32)


def dot_nt(left, right):
    return lax.dot_general(left, right, (((1,), (1,)), ((), ())), preferred_element_type=F32)


def transposed(rows):
    return jnp.transpose(rows.astype(F32))


def seq_bit(degree):
    return (lax.axis_index(SEQ_AXIS) >> degree) & 1 == 1


def call(
    body,
    out_shape,
    operands,
    scratch=(),
    flops=0,
    moved=0,
    in_space=pltpu.VMEM,
    out_space=pltpu.VMEM,
    limit=16 * 2**20,
):
    return pl.pallas_call(
        body,
        out_shape=out_shape,
        in_specs=[pl.BlockSpec(memory_space=in_space)] * len(operands),
        out_specs=jax.tree.map(lambda _: pl.BlockSpec(memory_space=out_space), out_shape),
        scratch_shapes=list(scratch),
        compiler_params=pltpu.CompilerParams(vmem_limit_bytes=limit),
        cost_estimate=pl.CostEstimate(flops=flops, bytes_accessed=moved, transcendentals=0),
    )(*operands)


def pack(members):
    rows, heads, width = members[0].shape
    count = len(members)
    members = [pltpu.with_memory_space_constraint(member, pltpu.HBM) for member in members]

    def body(*refs):
        ins, out = refs[:count], refs[count]
        narrow, sems = refs[count + 1 :]
        copies = [
            pltpu.make_async_copy(ins[index], narrow.at[index], sems.at[index])
            for index in range(count)
        ]
        for copy in copies:
            copy.start()
        for index in range(count):
            copies[index].wait()
            out[:, index * rows : (index + 1) * rows, :] = jnp.swapaxes(narrow[index], 0, 1)

    size = count * rows * heads * width
    return call(
        body,
        jax.ShapeDtypeStruct((heads, count * rows, width), BF16),
        members,
        [
            pltpu.VMEM((count, rows, heads, width), BF16),
            pltpu.SemaphoreType.DMA((count,)),
        ],
        moved=4 * size,
        in_space=pltpu.HBM,
        limit=16 * 2**20,
    )


def unpack(joined, grad_weights, count):
    heads, total, width = joined.shape
    rows = total // count

    def body(joined_ref, weight_ref, *refs):
        outs, weight_out = refs[:count], refs[count]
        narrow, sems = refs[count + 1 :]
        copies = [pltpu.make_async_copy(weight_ref, weight_out, sems.at[2 * count])]
        copies[0].start()
        for index in range(count):
            whole = jnp.swapaxes(joined_ref[:, index * rows : (index + 1) * rows, :], 0, 1)
            half = rows // 2
            for side in range(2):
                span = pl.ds(side * half, half)
                narrow[index, span] = whole[side * half : (side + 1) * half]
                copy = pltpu.make_async_copy(
                    narrow.at[index, span], outs[index].at[span], sems.at[2 * index + side]
                )
                copy.start()
                copies.append(copy)
        for copy in copies:
            copy.wait()

    size = count * rows * heads * width
    one = jax.ShapeDtypeStruct((rows, heads, width), BF16)
    return call(
        body,
        (one,) * count + (jax.ShapeDtypeStruct(grad_weights.shape, F32),),
        (joined, grad_weights),
        [
            pltpu.VMEM((count, rows, heads, width), BF16),
            pltpu.SemaphoreType.DMA((2 * count + 1,)),
        ],
        moved=4 * size,
        out_space=pltpu.HBM,
    )


def part(ref, index, chunk):
    sources, _, width = ref.shape
    return ref[:, index * chunk : (index + 1) * chunk, :].reshape(sources * chunk, width)


def block_states(rows_in, weights, chunk, first_far, far_count):
    width = rows_in.shape[2]

    def body(rows_ref, weight_ref, *message_refs):
        query, key, value, grad = (part(rows_ref, index, chunk) for index in range(4))
        query_t = transposed(query)
        pair = dot_nn(jnp.transpose(key), value)
        messages = []
        for degree in range(far_count):
            level = first_far + degree
            scale = level_factor(level, width) * weight_ref[level]
            state = dot_nn((scale * query_t).astype(BF16), grad)
            messages.append(jnp.where(seq_bit(degree), state, pair).astype(BF16))
        for refs, groups in zip(message_refs, SENT):
            for slot, degree in enumerate(groups):
                refs[slot] = messages[degree]

    shapes = tuple(jax.ShapeDtypeStruct((len(groups), width, width), BF16) for groups in SENT)
    return call(body, shapes, (rows_in, weights), flops=10**8, moved=10**6)


def near_terms(rows_in, weights, chunk, near_count):
    sources, _, width = rows_in.shape
    tokens = sources * chunk
    pieces = tokens // LANES
    inner = LANES.bit_length()

    def body(rows_ref, weight_ref, query_ref, key_ref, value_ref, grad_weight_ref):
        query, key, value, grad = (part(rows_ref, index, chunk) for index in range(4))
        scale = [level_factor(level, width) * weight_ref[level] for level in range(near_count)]
        source = lax.broadcasted_iota(jnp.int32, (LANES, LANES), 0)
        target = lax.broadcasted_iota(jnp.int32, (LANES, LANES), 1)
        crossed = source ^ target
        level_of = jnp.where(source <= target, 0, 64)
        for level in range(1, inner):
            level_of = level_of + (crossed >= 2 ** (level - 1)).astype(jnp.int32)
        masks = [level_of == level for level in range(inner)]
        sums = [[None] * pieces for _ in range(near_count)]
        key_t = transposed(key).astype(BF16)
        for low in range(pieces):
            begin = low * LANES
            scores = dot_nt(key[begin : begin + LANES], query[begin:])
            pulls = dot_nt(value[begin : begin + LANES], grad[begin:])
            product = scores * pulls
            inside = jnp.zeros((LANES, LANES), F32)
            corner = product[:, :LANES]
            for level in range(inner):
                row = scale[level][:, begin : begin + LANES]
                inside = jnp.where(masks[level], row, inside)
                sums[level][low] = jnp.sum(
                    jnp.where(masks[level], corner, 0.0), axis=0, keepdims=True
                )
            columns = [inside]
            for high in range(low + 1, pieces):
                level = (low ^ high).bit_length() + inner - 1
                left = (high - low) * LANES
                row = scale[level][:, high * LANES : (high + 1) * LANES]
                columns.append(jnp.broadcast_to(row, (LANES, LANES)))
                added = jnp.sum(product[:, left : left + LANES], axis=0, keepdims=True)
                held = sums[level][high]
                sums[level][high] = added if held is None else held + added
            weight = jnp.concatenate(columns, axis=1)
            scaled = (weight * scores).astype(BF16)
            pulled = (weight * pulls).astype(BF16)
            value_ref[begin : begin + LANES, :] = dot_nn(scaled, grad[begin:])
            key_ref[begin : begin + LANES, :] = dot_nn(pulled, query[begin:])
            partial = dot_nn(key_t[:, begin : begin + LANES], pulled)
            if low == 0:
                query_ref[...] = partial
            else:
                query_ref[:, begin:] = query_ref[:, begin:] + partial
        zero = jnp.zeros((1, LANES), F32)
        for level in range(near_count):
            row = jnp.concatenate([zero if item is None else item for item in sums[level]], axis=1)
            grad_weight_ref[level] = level_factor(level, width) * row

    return call(
        body,
        (
            jax.ShapeDtypeStruct((width, tokens), F32),
            jax.ShapeDtypeStruct((tokens, width), F32),
            jax.ShapeDtypeStruct((tokens, width), F32),
            jax.ShapeDtypeStruct((near_count, 1, tokens), F32),
        ),
        (rows_in, weights),
        flops=4 * 10**8,
        moved=3 * 10**6,
    )


def join_far(rows_in, weights, near, received, chunk, first_far, far_count):
    sources, _, width = rows_in.shape
    tokens = sources * chunk
    levels = weights.shape[0]
    query_near, key_near, value_near, weight_near = near

    def body(
        rows_ref,
        weight_ref,
        query_ref,
        key_ref,
        value_ref,
        near_weight_ref,
        *refs,
    ):
        message_refs, (out_ref, grad_weight_ref) = refs[:-2], refs[-2:]
        query, key, value, grad = (part(rows_ref, index, chunk) for index in range(4))
        sums = []
        for sources_of in TAKEN:
            terms = [message_refs[place][slot].astype(F32) for place, slot in sources_of]
            total = terms[0]
            for term in terms[1:]:
                total = total + term
            sums.append(total)
        query_t = transposed(query)
        total = query_ref[...]
        upper = jnp.zeros((width, width), F32)
        for degree in range(far_count):
            level = first_far + degree
            bit = seq_bit(degree)
            lower = jnp.where(bit, sums[degree], 0.0).astype(BF16)
            upper = upper + jnp.where(bit, 0.0, sums[degree])
            update = dot_nt(lower, grad)
            factor = level_factor(level, width)
            total = total + (factor * weight_ref[level]) * update
            grad_weight_ref[level] = factor * jnp.sum(query_t * update, axis=0, keepdims=True)
        for level in range(first_far):
            grad_weight_ref[level] = near_weight_ref[level]
        upper = upper.astype(BF16)
        results = (
            jnp.transpose(total.astype(BF16)),
            key_ref[...] + dot_nt(value, upper),
            value_ref[...] + dot_nn(key, upper),
        )
        for index, result in enumerate(results):
            out_ref[:, index * chunk : (index + 1) * chunk, :] = result.astype(BF16).reshape(
                sources, chunk, width
            )

    return call(
        body,
        (
            jax.ShapeDtypeStruct((sources, 3 * chunk, width), BF16),
            jax.ShapeDtypeStruct((levels, 1, tokens), F32),
        ),
        (rows_in, weights, query_near, key_near, value_near, weight_near, *received),
        flops=2 * 10**8,
        moved=3 * 10**6,
    )


def partner(value, mask):
    size = lax.axis_size(SEQ_AXIS)
    return lax.ppermute(value, SEQ_AXIS, [(place, place ^ mask) for place in range(size)])


def on_device(queries, keys, values, out_grad, level_weights):
    chunk = queries.shape[0]
    weights = jnp.transpose(level_weights, (1, 0, 2))
    sent = pack((queries, keys, values, out_grad))
    rows = lax.all_to_all(sent, HEAD_AXIS, 0, 0, tiled=True)
    first_far = weights.shape[2].bit_length()
    far_count = weights.shape[0] - first_far
    messages = block_states(rows, weights, chunk, first_far, far_count)
    near = near_terms(rows, weights, chunk, first_far)
    received = exchange(messages)
    joined, grad_weights = join_far(
        rows, weights, near, received, chunk, first_far, far_count
    )
    back = lax.all_to_all(joined, HEAD_AXIS, 0, 0, tiled=True)
    query_out, key_out, value_out, grad_weights = unpack(back, grad_weights, 3)
    return (query_out, key_out, value_out, jnp.transpose(grad_weights, (1, 0, 2)))


SENT = ((0, 2), (1,), (2,))
TAKEN = (((0, 0),), ((1, 0), (2, 0)), ((3, 0),))


def exchange(messages):
    a, b, c = messages
    near, mid, far = partner(a, 1), partner(c, 2), partner(c, 3)
    second, third = partner(b, 2), partner(b, 3)
    quad = c + near[1:] + mid + far
    return (near, second, third, partner(quad, 7))


def solution(mesh):
    rows = P((SEQ_AXIS, HEAD_AXIS), None, None)
    levels = P(HEAD_AXIS, None, SEQ_AXIS)

    return jax.shard_map(
        on_device,
        mesh=mesh,
        in_specs=(rows, rows, rows, rows, levels),
        out_specs=(rows, rows, rows, levels),
        check_vma=False,
    )
```
